32 devices in a mesh: seq: 8 (over z, x), head: 4 (over y, core).
Axes of the slice: x: 2, y: 2, z: 4, core: 2. Of those that a mesh axis runs over, the one named last changes fastest.
Arguments:
- query_input: bfloat16 [2048, 2048], P('seq', 'head'), may hold values from -6 to 6
- key_input: bfloat16 [2048, 2048], P('seq', 'head'), may hold values from -6 to 6
- value_input: bfloat16 [2048, 2048], P('seq', 'head'), may hold values from -6 to 6
- out_weight: bfloat16 [4096, 2048], P('seq', 'head'), may hold values from -0.125 to 0.125
- cotangent: bfloat16 [2048, 4096], P('seq', 'head'), may hold values from -6 to 6
Outputs:
- layer_out: bfloat16 [2048, 4096], P('seq', 'head')
- query_grad: bfloat16 [2048, 2048], P('seq', 'head')
- key_grad: bfloat16 [2048, 2048], P('seq', 'head')
- value_grad: bfloat16 [2048, 2048], P('seq', 'head')
- weight_grad: float32 [4096, 2048], P('seq', 'head')
The draws below stay inside these ranges and needn't reach their ends.
All inputs are finite; a program needn't handle non-finite values.
Results may differ from the reference program's by a relative error of at most 0.018.
Values may be sent and summed in bfloat16 or wider, within the bound.
No kernel may reach another device: no remote copies, remote signals or barrier semaphores. Data moves between devices by JAX's collectives and lax.ppermute only.
A program may use at most 128 MiB of HBM per device.

```python
import jax
import jax.numpy as jnp
from jax import lax

D = 4096
HEADS = 16
HEAD_DIM = 128
SEQ_LEN = 2048
BLOCK = 256
N_HEAD = 4


def raised(values, stream_key, source, target, blocks, factor):
    def block_of(position):
        return (jnp.arange(values.shape[position]) // (values.shape[position] // blocks)).reshape((-1,) + (1,) * (values.ndim - 1 - position))

    first = jax.random.permutation(stream_key, blocks)[block_of(target)]
    second = (block_of(target) + blocks // 2) % blocks
    return jnp.where((block_of(source) == first) | (block_of(source) == second), factor * values, values)


def block_levels(rng, shape, cuts, smallest, largest):
    def one(position, parts):
        draws = jax.random.uniform(jax.random.fold_in(jax.random.fold_in(rng, 6), position), (parts,), jnp.float32, smallest / len(cuts), largest / len(cuts))
        return jnp.repeat(jnp.exp(draws), shape[position] // parts).reshape((-1,) + (1,) * (len(shape) - position - 1))

    loudness = one(*cuts[0])
    for cut in cuts[1:]:
        loudness = loudness * one(*cut)
    return loudness


def scatter_about(stream_key, extent, scale, most, cuts=(), kind=jnp.bfloat16):
    array = scale * jax.random.normal(stream_key, extent, jnp.float32)
    if cuts:
        array = array * block_levels(stream_key, extent, cuts, -0.22, 0.18)
    return jnp.clip(array, -most, most).astype(kind)


def gaussian_with(stream_key, dims, spread, reach, cuts, heavy, kind=jnp.bfloat16):
    entries = spread * jax.random.normal(stream_key, dims, jnp.float32)
    if cuts:
        entries = entries * block_levels(stream_key, dims, cuts, -0.22, 0.18)
    return jnp.clip(raised(entries, jax.random.fold_in(stream_key, 3), *heavy), -reach, reach).astype(kind)


def setup_inputs(seed: int = 0) -> dict:
    streams_of = jax.random.split(jax.random.key(seed), 6)
    return {
        "query_input": scatter_about(streams_of[0], (SEQ_LEN, HEADS * HEAD_DIM), 1.0, 6.0, ((0, 8), (1, 4))),
        "key_input": scatter_about(streams_of[1], (SEQ_LEN, HEADS * HEAD_DIM), 1.0, 6.0, ((0, 8), (1, 4))),
        "value_input": scatter_about(streams_of[2], (SEQ_LEN, HEADS * HEAD_DIM), 1.0, 6.0, ((0, 8), (1, 4))),
        "out_weight": scatter_about(streams_of[3], (D, HEADS * HEAD_DIM), (HEADS * HEAD_DIM) ** -0.5, 0.125, ((0, 8), (1, 4))),
        "cotangent": gaussian_with(streams_of[4], (SEQ_LEN, D), 1.0, 6.0, ((0, 8), (1, 4)), (0, 1, 8, 2.0)),
    }


highest = lax.Precision.HIGHEST
epsilon = 1e-06

def features(raw_input):
    values = raw_input.astype(jnp.float32)
    return jnp.where(values > 0, values + 1.0, jnp.exp(jnp.minimum(values, 0.0)))

def feature_slope(raw_input):
    values = raw_input.astype(jnp.float32)
    return jnp.where(values > 0, 1.0, jnp.exp(jnp.minimum(values, 0.0)))

def reference(query_input, key_input, value_input, out_weight, cotangent):
    full_width = HEADS * HEAD_DIM
    block_total = SEQ_LEN // BLOCK

    def blocks_of(tensor_in):
        return tensor_in.reshape(block_total, BLOCK, HEADS, HEAD_DIM)
    q_feat = blocks_of(features(query_input).astype(jnp.bfloat16))
    k_feat = blocks_of(features(key_input).astype(jnp.bfloat16))
    v_vals = blocks_of(value_input)
    causal = jnp.tril(jnp.ones((BLOCK, BLOCK), jnp.float32))
    zero_state = jnp.zeros((HEADS, HEAD_DIM, HEAD_DIM), jnp.float32)

    def forward_step(carry_state, pieces):
        q_blk, k_blk, v_blk = pieces
        q_wide = q_blk.astype(jnp.float32)
        k_wide = k_blk.astype(jnp.float32)
        v_wide = v_blk.astype(jnp.float32)
        scores = (jnp.einsum('the,she->hts', q_wide, k_wide, precision=highest) * causal).astype(jnp.bfloat16)
        attended = jnp.einsum('hts,shf->thf', scores.astype(jnp.float32), v_wide, precision=highest)
        attended = attended + jnp.einsum('the,hef->thf', q_wide, carry_state, precision=highest)
        new_state = carry_state + jnp.einsum('the,thf->hef', k_wide, v_wide, precision=highest)
        return (new_state, (attended, carry_state, scores))
    final_state, (attended, prior_state, block_scores) = lax.scan(forward_step, zero_state, (q_feat, k_feat, v_vals))
    inv_rms = lax.rsqrt(lax.optimization_barrier(jnp.mean(attended * attended, axis=-1, keepdims=True)) + epsilon)
    unit_rms = attended * inv_rms
    normed = unit_rms.reshape(SEQ_LEN, full_width).astype(jnp.bfloat16)
    group_width = full_width // N_HEAD
    summed = jnp.zeros((SEQ_LEN, D), jnp.float32)
    for group_index in range(N_HEAD):
        low_col = group_index * group_width
        group_part = lax.dot_general(normed[:, low_col:low_col + group_width], out_weight[:, low_col:low_col + group_width], (((1,), (1,)), ((), ())), preferred_element_type=jnp.float32)
        rounded = lax.optimization_barrier(group_part.astype(jnp.bfloat16))
        summed = summed + rounded.astype(jnp.float32)
    layer_out = summed.astype(jnp.bfloat16)
    weight_grad = lax.dot_general(cotangent, normed, (((0,), (0,)), ((), ())), preferred_element_type=jnp.float32) * SEQ_LEN ** (-0.5)
    upstream = blocks_of(jnp.dot(cotangent, out_weight, preferred_element_type=jnp.float32))
    inner_term = lax.optimization_barrier(jnp.mean(upstream * unit_rms, axis=-1, keepdims=True))
    d_att = (inv_rms * (upstream - unit_rms * inner_term)).astype(jnp.bfloat16)

    def backward_step(after_state, pieces):
        q_blk, k_blk, v_blk, d_blk, carry_state, score_blk = pieces
        q_wide = q_blk.astype(jnp.float32)
        k_wide = k_blk.astype(jnp.float32)
        v_wide = v_blk.astype(jnp.float32)
        d_wide = d_blk.astype(jnp.float32)
        s_wide = score_blk.astype(jnp.float32)
        d_scores = (jnp.einsum('thf,shf->hts', d_wide, v_wide, precision=highest) * causal).astype(jnp.bfloat16).astype(jnp.float32)
        q_grad = jnp.einsum('hts,she->the', d_scores, k_wide, precision=highest)
        q_grad = q_grad + jnp.einsum('hef,thf->the', carry_state, d_wide, precision=highest)
        k_grad = jnp.einsum('hts,the->she', d_scores, q_wide, precision=highest)
        k_grad = k_grad + jnp.einsum('hef,shf->she', after_state, v_wide, precision=highest)
        v_grad = jnp.einsum('hts,thf->shf', s_wide, d_wide, precision=highest)
        v_grad = v_grad + jnp.einsum('hef,she->shf', after_state, k_wide, precision=highest)
        new_after = after_state + jnp.einsum('the,thf->hef', q_wide, d_wide, precision=highest)
        return (new_after, (q_grad, k_grad, v_grad))
    first_after, (q_grad, k_grad, v_grad) = lax.scan(backward_step, zero_state, (q_feat, k_feat, v_vals, d_att, prior_state, block_scores), reverse=True)
    query_grad = (q_grad * blocks_of(feature_slope(query_input))).reshape(SEQ_LEN, full_width).astype(jnp.bfloat16)
    key_grad = (k_grad * blocks_of(feature_slope(key_input))).reshape(SEQ_LEN, full_width).astype(jnp.bfloat16)
    value_grad = v_grad.reshape(SEQ_LEN, full_width).astype(jnp.bfloat16)
    return (layer_out, query_grad, key_grad, value_grad, weight_grad)
```

```python
import jax
import jax.numpy as jnp
from jax import lax
from jax.experimental import pallas as pl
from jax.experimental.pallas import tpu as pltpu
from jax.sharding import PartitionSpec as P

HEAD_DIM = 128


highest = lax.Precision.HIGHEST
epsilon = 1e-06
f32 = jnp.float32
bf16 = jnp.bfloat16


def features(raw_input):
    values = raw_input.astype(f32)
    return jnp.where(values > 0, values + 1.0, jnp.exp(jnp.minimum(values, 0.0)))


def feature_slope(raw_input):
    values = raw_input.astype(f32)
    return jnp.where(values > 0, 1.0, jnp.exp(jnp.minimum(values, 0.0)))


def running_sum(x, axis, backward):
    count = lax.axis_size(axis)
    place = lax.axis_index(axis)
    ahead = count - 1 - place if backward else place
    gathered = lax.all_gather(x.astype(bf16), axis)

    def one(turn, state):
        source = count - 1 - turn if backward else turn
        return state + lax.dynamic_index_in_dim(gathered, source, 0, False).astype(x.dtype)

    return lax.fori_loop(0, ahead, one, jnp.zeros_like(x))


def shards_any(query_input, key_input, value_input, out_weight, cotangent):
    row_count = query_input.shape[0]
    local_width = query_input.shape[1]
    heads_here = local_width // HEAD_DIM
    block_rows = min(512, row_count)
    block_count = row_count // block_rows

    def split_heads(tensor_in):
        return tensor_in.reshape(block_count, block_rows, heads_here, HEAD_DIM)

    q_feat = split_heads(features(query_input).astype(bf16))
    k_feat = split_heads(features(key_input).astype(bf16))
    v_vals = split_heads(value_input)
    block_states = jnp.einsum("bthe,bthf->bhef", k_feat, v_vals, preferred_element_type=f32)
    own_state = jnp.sum(block_states, axis=0)
    prefix = running_sum(own_state, "seq", False)
    prior_state = prefix[None] + jnp.cumsum(block_states, axis=0) - block_states
    causal = jnp.tril(jnp.ones((block_rows, block_rows), f32))
    scores = (
        jnp.einsum("bthe,bshe->bhts", q_feat, k_feat, preferred_element_type=f32) * causal
    ).astype(bf16)
    attended = jnp.einsum("bhts,bshf->bthf", scores, v_vals, preferred_element_type=f32)
    attended = attended + jnp.einsum(
        "bthe,bhef->bthf", q_feat.astype(f32), prior_state, precision=highest
    )
    inv_rms = lax.rsqrt(jnp.mean(attended * attended, axis=-1, keepdims=True) + epsilon)
    unit_rms = attended * inv_rms
    normed = unit_rms.reshape(row_count, local_width).astype(bf16)
    dy_whole = lax.all_gather(cotangent, "head", axis=1, tiled=True)
    w_whole = lax.all_gather(out_weight, "seq", axis=0, tiled=True)
    partial_value = lax.dot_general(
        normed, w_whole, (((1,), (1,)), ((), ())), preferred_element_type=f32
    )
    upstream = jnp.dot(dy_whole, w_whole, preferred_element_type=f32)
    layer_out = lax.psum_scatter(
        partial_value.astype(bf16), "head", scatter_dimension=1, tiled=True
    )
    grad_scale = (row_count * lax.axis_size("seq")) ** (-0.5)
    weight_grad = (
        lax.psum_scatter(
            lax.dot_general(dy_whole, normed, (((0,), (0,)), ((), ())), preferred_element_type=f32),
            "seq",
            scatter_dimension=0,
            tiled=True,
        )
        * grad_scale
    )
    d_unit = split_heads(upstream)
    inner_term = jnp.mean(d_unit * unit_rms, axis=-1, keepdims=True)
    d_att = (inv_rms * (d_unit - unit_rms * inner_term)).astype(bf16)
    block_adjoint = jnp.einsum("bthe,bthf->bhef", q_feat, d_att, preferred_element_type=f32)
    own_adjoint = jnp.sum(block_adjoint, axis=0)
    suffix = running_sum(own_adjoint, "seq", True)
    after_state = suffix[None] + own_adjoint[None] - jnp.cumsum(block_adjoint, axis=0)
    d_scores = (
        jnp.einsum("bthf,bshf->bhts", d_att, v_vals, preferred_element_type=f32) * causal
    ).astype(bf16)
    q_grad = jnp.einsum("bhts,bshe->bthe", d_scores, k_feat, preferred_element_type=f32)
    q_grad = q_grad + jnp.einsum(
        "bhef,bthf->bthe", prior_state, d_att.astype(f32), precision=highest
    )
    k_grad = jnp.einsum("bhts,bthe->bshe", d_scores, q_feat, preferred_element_type=f32)
    k_grad = k_grad + jnp.einsum(
        "bhef,bshf->bshe", after_state, v_vals.astype(f32), precision=highest
    )
    v_grad = jnp.einsum("bhts,bthf->bshf", scores, d_att, preferred_element_type=f32)
    v_grad = v_grad + jnp.einsum(
        "bhef,bshe->bshf", after_state, k_feat.astype(f32), precision=highest
    )
    query_grad = (
        (q_grad * split_heads(feature_slope(query_input)))
        .reshape(row_count, local_width)
        .astype(bf16)
    )
    key_grad = (
        (k_grad * split_heads(feature_slope(key_input)))
        .reshape(row_count, local_width)
        .astype(bf16)
    )
    value_grad = v_grad.reshape(row_count, local_width).astype(bf16)
    return (layer_out, query_grad, key_grad, value_grad, weight_grad)


def bits():
    place = lax.axis_index("seq")
    lane = lax.axis_index("head")
    return place // 4, (place // 2) % 2, place % 2, lane // 2, lane % 2


def dot(a, b, ca, cb):
    return lax.dot_general(a, b, (((ca,), (cb,)), ((), ())), preferred_element_type=f32)


def split_dot(a, b, cb):
    high = b.astype(bf16)
    low = (b - high.astype(f32)).astype(bf16)
    return dot(a, high, 1, cb) + dot(a, low, 1, cb)


def call(body, outs, args, name, flops, scratch=()):
    vmem = pl.BlockSpec(memory_space=pltpu.VMEM)
    smem = pl.BlockSpec(memory_space=pltpu.SMEM)
    size = sum(x.size * x.dtype.itemsize for x in tuple(args) + tuple(outs))
    return pl.pallas_call(
        body,
        out_shape=outs,
        in_specs=[smem if a.ndim == 1 else vmem for a in args],
        out_specs=[vmem for _ in outs],
        scratch_shapes=list(scratch),
        name=name,
        cost_estimate=pl.CostEstimate(flops=flops, bytes_accessed=size, transcendentals=0),
    )(*args)


def like(shape, kind):
    return jax.ShapeDtypeStruct(shape, kind)


def shards_cube(query_input, key_input, value_input, out_weight, cotangent):
    rows, width = query_input.shape
    heads = width // HEAD_DIM
    w_rows = out_weight.shape[0]
    far, near, side, pair, core = bits()
    cut = [slice(h * HEAD_DIM, (h + 1) * HEAD_DIM) for h in range(heads)]
    states = (heads, HEAD_DIM, HEAD_DIM)
    flags = jnp.where(
        lax.iota(jnp.int32, 8) == 0,
        near ^ core,
        jnp.where(
            lax.iota(jnp.int32, 8) == 1,
            far ^ pair,
            jnp.where(
                lax.iota(jnp.int32, 8) == 2,
                side,
                jnp.where(lax.iota(jnp.int32, 8) == 3, near, far),
            ),
        ),
    )
    tri = (256 * rows * rows * HEAD_DIM * heads) // 256

    def seq_swap(x, mask):
        return lax.ppermute(x, "seq", [(i, i ^ mask) for i in range(8)])

    def head_swap(x, mask):
        return lax.ppermute(x, "head", [(i, i ^ mask) for i in range(4)])

    def cross(x, flip):
        moves = []
        for s in range(8):
            for j in range(4):
                n, c = (s >> 1) & 1, j & 1
                to_s = (s & 4) | (c << 1) | ((s & 1) ^ flip)
                to_j = (j & 2) | n
                moves.append((s * 4 + j, to_s * 4 + to_j))
        return lax.ppermute(x, ("seq", "head"), moves)

    half = w_rows
    cot_same = lax.dynamic_slice(cotangent, (0, side * half), (rows, half))
    cot_other = lax.dynamic_slice(cotangent, (0, (1 - side) * half), (rows, half))
    a0 = cross(cot_same, 0)
    a1 = cross(cot_other, 1)
    w_far = seq_swap(out_weight, 4)

    def state_body(k_ref, v_ref, kf_ref, s16_ref, s32_ref):
        for h in range(heads):
            kf = features(k_ref[:, cut[h]]).astype(bf16)
            kf_ref[:, cut[h]] = kf
            s = dot(kf, v_ref[:, cut[h]], 0, 0)
            s32_ref[h] = s
            s16_ref[h] = s.astype(bf16)

    k_feat, own16, own32 = call(
        state_body,
        [like((rows, width), bf16), like(states, bf16), like(states, f32)],
        [key_input, value_input],
        "state",
        2 * rows * width * HEAD_DIM,
    )

    def scan(own16, own32, backward):
        r0 = seq_swap(own16, 1)
        both = own32 + r0.astype(f32)
        r1 = seq_swap(both.astype(bf16), 2)
        four = (both + r1.astype(f32)).astype(bf16)
        moves = [(s + 4, s) if backward else (s, s + 4) for s in range(4)]
        r2 = lax.ppermute(four, "seq", moves)
        return r0, r1, r2

    p0, p1, p2 = scan(own16, own32, False)

    b0 = head_swap(a0, 2)
    b1 = head_swap(a1, 2)
    ac0 = head_swap(a0, 1)
    ac1 = head_swap(a1, 1)
    bc0 = head_swap(b0, 1)
    bc1 = head_swap(b1, 1)

    def causal_mask():
        t = lax.broadcasted_iota(jnp.int32, (rows, rows), 0)
        s = lax.broadcasted_iota(jnp.int32, (rows, rows), 1)
        return s <= t

    def inside_body(q_ref, kf_ref, v_ref, qf_ref, sc_ref, att_ref):
        mask = causal_mask()
        for h in range(heads):
            qf = features(q_ref[:, cut[h]]).astype(bf16)
            qf_ref[:, cut[h]] = qf
            sc = jnp.where(mask, dot(qf, kf_ref[:, cut[h]], 1, 1), 0.0).astype(bf16)
            sc_ref[h] = sc
            att_ref[:, cut[h]] = dot(sc, v_ref[:, cut[h]], 1, 0)

    q_feat, scores, inside = call(
        inside_body,
        [like((rows, width), bf16), like((heads, rows, rows), bf16), like((rows, width), f32)],
        [query_input, k_feat, value_input],
        "inside",
        4 * tri,
    )

    def norm_body(flag_ref, p0_ref, p1_ref, p2_ref, qf_ref, in_ref, att_ref, norm_ref, prior_ref):
        for h in range(heads):
            prior = jnp.where(flag_ref[2] == 1, p0_ref[h].astype(f32), 0.0)
            prior = prior + jnp.where(flag_ref[3] == 1, p1_ref[h].astype(f32), 0.0)
            prior = prior + jnp.where(flag_ref[4] == 1, p2_ref[h].astype(f32), 0.0)
            prior_ref[h] = prior
            att = in_ref[:, cut[h]] + split_dot(qf_ref[:, cut[h]], prior, 0)
            att_ref[:, cut[h]] = att
            inv = lax.rsqrt(jnp.mean(att * att, axis=-1, keepdims=True) + epsilon)
            norm_ref[:, cut[h]] = (att * inv).astype(bf16)

    attended, normed, prior = call(
        norm_body,
        [like((rows, width), f32), like((rows, width), bf16), like(states, f32)],
        [flags, p0, p1, p2, q_feat, inside],
        "norm",
        4 * rows * width * HEAD_DIM,
    )
    n_side = seq_swap(normed, 1)
    n_near = seq_swap(normed, 2)
    n_both = seq_swap(normed, 3)

    def up_body(flag_ref, *refs):
        cots, (w_own, w_far_ref), outs, w = refs[:8], refs[8:10], refs[10:14], refs[14]
        w[0] = w_own[...]
        w[1] = w_far_ref[...]
        e, f = flag_ref[0], flag_ref[1]
        for c in range(2):
            for s in range(2):
                part = dot(cots[c * 2 + s][...], w[f], 1, 0)
                part = part + dot(cots[4 + c * 2 + s][...], w[1 - f], 1, 0)

                @pl.when((e ^ c) == 0)
                def _(part=part, s=s):
                    outs[s][...] = part.astype(outs[s].dtype)

                @pl.when((e ^ c) == 1)
                def _(part=part, s=s):
                    outs[2 + s][...] = part.astype(outs[2 + s].dtype)

    cots = [a0, a1, ac0, ac1, b0, b1, bc0, bc1]
    box = 2 * 4 * rows * 2 * w_rows * width
    u_own, u_side, u_near, u_both = call(
        up_body,
        [like((rows, width), f32)] + [like((rows, width), bf16)] * 3,
        [flags] + cots + [out_weight, w_far],
        "up",
        box,
        [pltpu.VMEM((2, w_rows, width), bf16)],
    )
    u_side = seq_swap(u_side, 1)
    u_near = seq_swap(u_near, 2)
    u_both = seq_swap(u_both, 3)

    def out_body(flag_ref, n0, n1, n2, n3, w_own, w_far_ref, keep_ref, send_ref):
        e, f = flag_ref[0], flag_ref[1]
        ns = (n0, n1, n2, n3)
        for w, w_ref in ((0, w_own), (1, w_far_ref)):
            for l in range(2):
                for s in range(2):
                    part = dot(ns[l * 2 + s][...], w_ref[...], 1, 1).astype(bf16)

                    @pl.when((e ^ l) == 0)
                    def _(part=part, s=s, w=w):
                        keep_ref[f ^ w, s] = part

                    @pl.when((e ^ l) == 1)
                    def _(part=part, s=s, w=w):
                        send_ref[f ^ w, s] = part

    norms = [normed, n_side, n_near, n_both]
    keep, send = call(
        out_body,
        [like((2, 2, rows, w_rows), bf16)] * 2,
        [flags] + norms + [out_weight, w_far],
        "out",
        box,
    )
    from_core = head_swap(send, 1)
    pair_send = (keep[1].astype(f32) + from_core[1].astype(f32)).astype(bf16)
    from_pair = head_swap(pair_send, 2)
    total = (keep[0].astype(f32) + from_core[0].astype(f32) + from_pair.astype(f32)).astype(bf16)
    o_same = cross(total[0], 0)
    o_other = cross(total[1], 1)
    layer_out = jnp.concatenate(
        [jnp.where(side == 0, o_same, o_other), jnp.where(side == 0, o_other, o_same)], axis=1
    )

    def grad_body(flag_ref, *refs):
        cots, ns, (keep_ref, send_ref), stack = refs[:8], refs[8:12], refs[12:14], refs[14]
        for i in range(4):
            stack[i] = ns[i][...]
        e, f = flag_ref[0], flag_ref[1]
        for d in range(2):
            part = None
            for c in range(2):
                for s in range(2):
                    one = dot(cots[d * 4 + c * 2 + s][...], stack[(e ^ c) * 2 + s], 0, 0)
                    part = one if part is None else part + one

            @pl.when(f == d)
            def _(part=part):
                keep_ref[...] = part

            @pl.when(f != d)
            def _(part=part):
                send_ref[...] = part.astype(bf16)

    g_keep, g_send = call(
        grad_body,
        [like((w_rows, width), f32), like((w_rows, width), bf16)],
        [flags] + cots + norms,
        "grad",
        box,
        [pltpu.VMEM((4, rows, width), bf16)],
    )
    g_far = seq_swap(g_send, 4)
    grad_scale = (rows * 8) ** (-0.5)
    weight_grad = (g_keep + g_far.astype(f32)) * grad_scale

    def adj_body(u0, u1, u2, u3, att_ref, qf_ref, d_ref, s16_ref, s32_ref):
        for h in range(heads):
            up = u0[:, cut[h]] + u1[:, cut[h]].astype(f32)
            up = up + u2[:, cut[h]].astype(f32) + u3[:, cut[h]].astype(f32)
            att = att_ref[:, cut[h]]
            inv = lax.rsqrt(jnp.mean(att * att, axis=-1, keepdims=True) + epsilon)
            unit = att * inv
            inner = jnp.mean(up * unit, axis=-1, keepdims=True)
            d = (inv * (up - unit * inner)).astype(bf16)
            d_ref[:, cut[h]] = d
            s = dot(qf_ref[:, cut[h]], d, 0, 0)
            s32_ref[h] = s
            s16_ref[h] = s.astype(bf16)

    d_att, adj16, adj32 = call(
        adj_body,
        [like((rows, width), bf16), like(states, bf16), like(states, f32)],
        [u_own, u_side, u_near, u_both, attended, q_feat],
        "adj",
        2 * rows * width * HEAD_DIM,
    )
    s0, s1, s2 = scan(adj16, adj32, True)

    def back_body(d_ref, v_ref, kf_ref, qf_ref, sc_ref, prior_ref, q_ref, qg_ref, kg_ref, vg_ref):
        mask = causal_mask()
        for h in range(heads):
            d = d_ref[:, cut[h]]
            ds = jnp.where(mask, dot(d, v_ref[:, cut[h]], 1, 1), 0.0).astype(bf16)
            qg = dot(ds, kf_ref[:, cut[h]], 1, 0) + split_dot(d, prior_ref[h], 1)
            qg_ref[:, cut[h]] = (qg * feature_slope(q_ref[:, cut[h]])).astype(bf16)
            kg_ref[:, cut[h]] = dot(ds, qf_ref[:, cut[h]], 0, 0)
            vg_ref[:, cut[h]] = dot(sc_ref[h], d, 0, 0)

    query_grad, k_part, v_part = call(
        back_body,
        [like((rows, width), bf16), like((rows, width), f32), like((rows, width), f32)],
        [d_att, value_input, k_feat, q_feat, scores, prior, query_input],
        "back",
        8 * tri,
    )

    def last_body(flag_ref, s0_ref, s1_ref, s2_ref, v_ref, kf_ref, k_ref, kp, vp, kg_ref, vg_ref):
        for h in range(heads):
            after = jnp.where(flag_ref[2] == 0, s0_ref[h].astype(f32), 0.0)
            after = after + jnp.where(flag_ref[3] == 0, s1_ref[h].astype(f32), 0.0)
            after = after + jnp.where(flag_ref[4] == 0, s2_ref[h].astype(f32), 0.0)
            kg = kp[:, cut[h]] + split_dot(v_ref[:, cut[h]], after, 1)
            kg_ref[:, cut[h]] = (kg * feature_slope(k_ref[:, cut[h]])).astype(bf16)
            vg = vp[:, cut[h]] + split_dot(kf_ref[:, cut[h]], after, 0)
            vg_ref[:, cut[h]] = vg.astype(bf16)

    key_grad, value_grad = call(
        last_body,
        [like((rows, width), bf16)] * 2,
        [flags, s0, s1, s2, value_input, k_feat, key_input, k_part, v_part],
        "last",
        8 * rows * width * HEAD_DIM,
    )
    return (layer_out, query_grad, key_grad, value_grad, weight_grad)


def solution(mesh):
    spec = P("seq", "head")
    cube = mesh.shape["seq"] == 8 and mesh.shape["head"] == 4
    return jax.shard_map(
        shards_cube if cube else shards_any,
        mesh=mesh,
        in_specs=(spec,) * 5,
        out_specs=(spec,) * 5,
        check_vma=False,
    )
```
